32 devices in a mesh: dp: 8 (over z, core), space: 4 (over y, x).
Axes of the slice: x: 2, y: 2, z: 4, core: 2. Of those that a mesh axis runs over, the one named last changes fastest.
Arguments:
- fields: bfloat16 [8, 8, 96, 128], P('dp', 'space'), may hold values from -6 to 6
- cotangent: bfloat16 [8, 8, 96, 128], P('dp', 'space'), may hold values from -6 to 6
- weights: bfloat16 [2, 1152, 128], replicated, may hold values from -6 to 6
- master: float32 [2, 147456], P(None, ('dp', 'space')), may hold values from -6 to 6
- momentum: float32 [2, 147456], P(None, ('dp', 'space')), may hold values from -6 to 6
Outputs:
- result_fields: bfloat16 [8, 8, 96, 128], P('dp', 'space')
- input_grad: bfloat16 [8, 8, 96, 128], P('dp', 'space')
- momentum_next: float32 [2, 147456], P(None, ('dp', 'space'))
- master_next: float32 [2, 147456], P(None, ('dp', 'space'))
- weights_next: bfloat16 [2, 1152, 128], replicated
The draws below stay inside these ranges and needn't reach their ends.
All inputs are finite; a program needn't handle non-finite values.
Results may differ from the reference program's by a relative error of at most 0.006.
Values may be sent and summed in bfloat16 or wider, within the bound.
No kernel may reach another device: no remote copies, remote signals or barrier semaphores. Data moves between devices by JAX's collectives and lax.ppermute only.
A program may use at most 64 MiB of HBM per device.

```python
import jax
import jax.numpy as jnp
from jax import lax

C = 128
LAYERS = 2
COLS = 96
SAMPLES = 8
HEIGHT = 8
PIXELS = 6144


def levels(own_key, extent, shards, least, top_value):
    gain = 1.0
    for dim, shards_of in shards:
        draws = jax.random.uniform(jax.random.fold_in(jax.random.fold_in(own_key, 6), dim), (shards_of,), jnp.float32, least / len(shards), top_value / len(shards))
        gain = gain * jnp.repeat(jnp.exp(draws), extent[dim] // shards_of).reshape((-1,) + (1,) * (len(extent) - 1 - dim))
    return gain


def centred(own_key, extent, scale, most, cuts=(), dtype=jnp.bfloat16):
    values = scale * jax.random.normal(own_key, extent, jnp.float32)
    if cuts:
        values = values * levels(own_key, extent, cuts, -0.22, 0.18)
    return jnp.clip(values, -most, most).astype(dtype)


def setup_inputs(seed: int = 0) -> dict:
    key_list = jax.random.split(jax.random.key(seed), 6)
    return {
        "fields": centred(key_list[0], (SAMPLES, HEIGHT, COLS, C), 1.0, 6.0, ((0, 8), (1, 4))),
        "cotangent": centred(key_list[1], (SAMPLES, HEIGHT, COLS, C), 1.0, 6.0, ((0, 8), (1, 4))),
        "weights": centred(key_list[2], (LAYERS, 9 * C, C), 1.0, 6.0),
        "master": centred(key_list[3], (LAYERS, 9 * C * C), 1.0, 6.0, ((1, 32),), jnp.float32),
        "momentum": centred(key_list[4], (LAYERS, 9 * C * C), 1.0, 6.0, ((1, 32),), jnp.float32),
    }


momentum_rate = 0.9
learn_rate = 0.1

def taps(padded, dilation, height, col_count):
    channels = padded.shape[-1]
    padded = jnp.pad(padded, ((0, 0), (dilation, dilation), (0, 0)))
    pieces = [padded[tap_row * dilation:tap_row * dilation + height, tap_col * dilation:tap_col * dilation + col_count, :] for tap_row in range(3) for tap_col in range(3)]
    return jnp.concatenate(pieces, axis=-1).reshape(height * col_count, 9 * channels)

def flipped(kernel):
    channels = kernel.shape[-1]
    return kernel.reshape(3, 3, channels, channels)[::-1, ::-1].transpose(0, 1, 3, 2).reshape(9 * channels, channels)

def swish_slope(pre_act):
    sigmoid_value = jax.nn.sigmoid(pre_act)
    return sigmoid_value * (1.0 + pre_act * (1.0 - sigmoid_value))

def contract_rows(left_mat, right_mat):
    return lax.dot_general(left_mat, right_mat, (((0,), (0,)), ((), ())), preferred_element_type=jnp.float32)

def sample_step(fields, cotangent, weights):
    height, col_count, channels = fields.shape
    fan_scale = (9.0 * channels) ** (-0.5)

    def padder(array, depth):
        return jnp.pad(array, ((depth, depth), (0, 0), (0, 0)))
    inner_taps = taps(padder(fields, 1), 1, height, col_count)
    pre_one = jnp.dot(inner_taps, weights[0], preferred_element_type=jnp.float32) * fan_scale
    hidden = jax.nn.silu(pre_one).astype(jnp.bfloat16)
    outer_taps = taps(padder(hidden.reshape(height, col_count, channels), 2), 2, height, col_count)
    pre_two = jnp.dot(outer_taps, weights[1], preferred_element_type=jnp.float32) * fan_scale
    flat_cot = cotangent.reshape(height * col_count, channels).astype(jnp.float32)
    result = (jax.nn.silu(pre_two) + hidden.astype(jnp.float32)).astype(jnp.bfloat16)
    delta_two = (flat_cot * swish_slope(pre_two)).astype(jnp.bfloat16)
    back_two = taps(padder(delta_two.reshape(height, col_count, channels), 2), 2, height, col_count)
    mid_grad = jnp.dot(back_two, flipped(weights[1]), preferred_element_type=jnp.float32) * fan_scale + flat_cot
    delta_one = (mid_grad * swish_slope(pre_one)).astype(jnp.bfloat16)
    back_one = taps(padder(delta_one.reshape(height, col_count, channels), 1), 1, height, col_count)
    input_grad = (jnp.dot(back_one, flipped(weights[0]), preferred_element_type=jnp.float32) * fan_scale).astype(jnp.bfloat16)
    grad_one = contract_rows(inner_taps, delta_one) * fan_scale
    grad_two = contract_rows(outer_taps, delta_two) * fan_scale
    return (result.reshape(height, col_count, channels), input_grad.reshape(height, col_count, channels), jnp.stack([grad_one, grad_two]))

def reference(fields, cotangent, weights, master, momentum):

    def accumulate(summed, sample_pair):
        result, input_grad, grads = sample_step(sample_pair[0], sample_pair[1], weights)
        return (summed + grads, (result, input_grad))
    summed, (results, input_grads) = lax.scan(accumulate, jnp.zeros((LAYERS, 9 * C, C), jnp.float32), (fields, cotangent))
    gradient = (summed * jnp.sqrt(jnp.float32(9.0 * C / PIXELS))).reshape(LAYERS, 9 * C * C)
    momentum_next = momentum_rate * momentum + gradient
    master_next = master - learn_rate * momentum_next
    weights_next = master_next.astype(jnp.bfloat16).reshape(LAYERS, 9 * C, C)
    return (results, input_grads, momentum_next, master_next, weights_next)
```

```python
import jax
import jax.numpy as jnp
from jax import lax
from jax.sharding import PartitionSpec as P

momentum_rate = 0.9
learn_rate = 0.1


def taps(rows, dilation):
    height, col_count, channels = rows.shape
    padded = jnp.pad(rows, ((dilation, dilation), (dilation, dilation), (0, 0)))
    pieces = [
        padded[
            tap_row * dilation : tap_row * dilation + height,
            tap_col * dilation : tap_col * dilation + col_count,
            :,
        ]
        for tap_row in range(3)
        for tap_col in range(3)
    ]
    return jnp.concatenate(pieces, axis=-1).reshape(height * col_count, 9 * channels)


def flipped(kernel):
    channels = kernel.shape[-1]
    return (
        kernel.reshape(3, 3, channels, channels)[::-1, ::-1]
        .transpose(0, 1, 3, 2)
        .reshape(9 * channels, channels)
    )


def swish_slope(pre_act):
    sigmoid_value = jax.nn.sigmoid(pre_act)
    return sigmoid_value * (1.0 + pre_act * (1.0 - sigmoid_value))


def contract_rows(left_mat, right_mat):
    return lax.dot_general(
        left_mat, right_mat, (((0,), (0,)), ((), ())), preferred_element_type=jnp.float32
    )


def local(fields, cotangent, weights, master, momentum):
    _, strip, col_count, channels = fields.shape
    layers = weights.shape[0]
    dp_count = lax.axis_size("dp")
    space_count = lax.axis_size("space")
    height = strip * space_count
    cells = height * col_count
    where = lax.axis_index("space")
    fan_scale = (9.0 * channels) ** (-0.5)

    both = lax.all_gather(jnp.concatenate([fields, cotangent], axis=0), "space", axis=0)
    sample = both[:, 0].reshape(height, col_count, channels)
    flat_cot = both[:, 1].reshape(cells, channels).astype(jnp.float32)

    def own(flat):
        return lax.dynamic_slice_in_dim(flat, where * strip * col_count, strip * col_count, axis=0)

    inner_taps = taps(sample, 1)
    pre_one = jnp.dot(inner_taps, weights[0], preferred_element_type=jnp.float32) * fan_scale
    hidden = jax.nn.silu(pre_one).astype(jnp.bfloat16)
    outer_taps = taps(hidden.reshape(height, col_count, channels), 2)
    pre_two = jnp.dot(outer_taps, weights[1], preferred_element_type=jnp.float32) * fan_scale
    result = (jax.nn.silu(pre_two) + hidden.astype(jnp.float32)).astype(jnp.bfloat16)
    delta_two = (flat_cot * swish_slope(pre_two)).astype(jnp.bfloat16)
    back_two = taps(delta_two.reshape(height, col_count, channels), 2)
    mid_grad = (
        jnp.dot(back_two, flipped(weights[1]), preferred_element_type=jnp.float32) * fan_scale
        + flat_cot
    )
    delta_one = (mid_grad * swish_slope(pre_one)).astype(jnp.bfloat16)
    back_one = taps(delta_one.reshape(height, col_count, channels), 1)
    input_grad = (
        jnp.dot(own(back_one), flipped(weights[0]), preferred_element_type=jnp.float32) * fan_scale
    ).astype(jnp.bfloat16)
    grad_one = contract_rows(inner_taps, delta_one)
    grad_two = contract_rows(outer_taps, delta_two)

    pixel_total = dp_count * fields.shape[0] * cells
    grad_factor = fan_scale * (9.0 * channels / pixel_total) ** 0.5
    shard_len = 9 * channels * channels // (dp_count * space_count)
    blocks = (jnp.stack([grad_one, grad_two]) * grad_factor).astype(jnp.bfloat16)
    blocks = blocks.reshape(layers, dp_count, space_count, shard_len)
    quarter = lax.dynamic_index_in_dim(blocks, where, axis=2, keepdims=False)
    swapped = lax.all_to_all(quarter.transpose(1, 0, 2), "dp", 0, 0, tiled=True)
    gradient = swapped.astype(jnp.float32).sum(axis=0)
    momentum_next = momentum_rate * momentum + gradient
    master_next = master - learn_rate * momentum_next
    pieces = lax.all_gather(master_next.astype(jnp.bfloat16), ("dp", "space"), axis=0)
    weights_next = pieces.transpose(1, 0, 2).reshape(layers, 9 * channels, channels)
    return (
        own(result).reshape(1, strip, col_count, channels),
        input_grad.reshape(1, strip, col_count, channels),
        momentum_next,
        master_next,
        weights_next,
    )


def solution(mesh):
    split = P("dp", "space", None, None)
    shard = P(None, ("dp", "space"))
    return jax.shard_map(
        local,
        mesh=mesh,
        in_specs=(split, split, P(), shard, shard),
        out_specs=(split, split, shard, shard, P()),
        check_vma=False,
    )
```

```python
import functools

import jax
import jax.numpy as jnp
from jax import lax
from jax.experimental import pallas as pl
from jax.experimental.pallas import tpu as pltpu
from jax.sharding import PartitionSpec as P

momentum_rate = 0.9
learn_rate = 0.1
lane = 128


def sigmoid(value):
    return 1.0 / (1.0 + jnp.exp(-value))


def slope_of(value, sig):
    return sig * (1.0 + value * (1.0 - sig))


def spread(rows, shift_ref, dilation, height, cols):
    channels = rows.shape[-1]
    cube = rows.reshape(height, cols, channels)
    column = lax.broadcasted_iota(jnp.int32, cube.shape, 1)
    margin = dilation * cols
    right = jnp.where(column < dilation, 0.0, pltpu.roll(cube, dilation, 1))
    left = jnp.where(column >= cols - dilation, 0.0, pltpu.roll(cube, cols - dilation, 1))
    for b, moved in enumerate((right, cube, left)):
        lanes = slice(b * channels, (b + 1) * channels)
        shift_ref[margin : margin + height * cols, lanes] = moved.reshape(
            height * cols, channels
        ).astype(jnp.bfloat16)
    edge = jnp.zeros((margin, 3 * channels), jnp.bfloat16)
    shift_ref[:margin, :] = edge
    shift_ref[margin + height * cols : 2 * margin + height * cols, :] = edge


def conv(shift_ref, kernel_ref, layer, dilation, cells, cols, channels):
    total = None
    for a in range(3):
        part = jnp.dot(
            shift_ref[a * dilation * cols : a * dilation * cols + cells, :],
            kernel_ref[layer, a * 3 * channels : (a + 1) * 3 * channels, :],
            preferred_element_type=jnp.float32,
        )
        total = part if total is None else total + part
    return total


def back_conv(shift_ref, flip_ref, dilation, cells, cols):
    total = None
    for a in range(3):
        part = lax.dot_general(
            shift_ref[a * dilation * cols : a * dilation * cols + cells, :],
            flip_ref[a],
            (((1,), (1,)), ((), ())),
            preferred_element_type=jnp.float32,
        )
        total = part if total is None else total + part
    return total


def flip_into(kernel_ref, layer, flip_ref, channels):
    for a in range(3):
        for b in range(3):
            tap = ((2 - a) * 3 + (2 - b)) * channels
            flip_ref[a, :, b * channels : (b + 1) * channels] = kernel_ref[
                layer, tap : tap + channels, :
            ]


def map_grad(shift_ref, delta, grad_ref, base, dilation, cells, cols, channels, factor):
    for a in range(3):
        part = lax.dot_general(
            shift_ref[a * dilation * cols : a * dilation * cols + cells, :],
            delta,
            (((0,), (0,)), ((), ())),
            preferred_element_type=jnp.float32,
        )
        start = base + a * 3 * channels
        grad_ref[start : start + 3 * channels, :] = part * factor


def step_kernel(plan, *refs):
    count, strip, cols, channels, fan_scale, factor, split = plan
    pieces, kernel_ref = (refs[:count], refs[count])
    if split:
        result_ref, input_ref, send_ref, keep_ref = refs[count + 1 : count + 5]
        scratch = refs[count + 5 :]
    else:
        result_ref, input_ref, grad_out = refs[count + 1 : count + 4]
        scratch = refs[count + 4 :]
    sample, cot, shift_one, shift_two, shift_back, flip, pre, grad, stage = scratch
    height, rows = (count * strip, strip * cols)
    cells = height * cols
    where = lax.axis_index("space")
    for k in range(count):
        spot = (where ^ k) if split else k
        place = pl.ds(pl.multiple_of(spot * rows, rows), rows)
        sample[place, :] = pieces[k][0].astype(jnp.float32)
        cot[place, :] = pieces[k][1].astype(jnp.float32)

    spread(sample[...], shift_one, 1, height, cols)
    pre_one = conv(shift_one, kernel_ref, 0, 1, cells, cols, channels) * fan_scale
    sig = sigmoid(pre_one)
    slope_one = slope_of(pre_one, sig)
    hidden = (pre_one * sig).astype(jnp.bfloat16).astype(jnp.float32)
    sample[...] = hidden
    spread(hidden, shift_two, 2, height, cols)
    pre_two = conv(shift_two, kernel_ref, 1, 2, cells, cols, channels) * fan_scale
    sig = sigmoid(pre_two)
    pre[...] = pre_two * sig
    own = pl.ds(pl.multiple_of(where * rows, rows), rows)
    result_ref[...] = (pre[own, :] + sample[own, :]).astype(jnp.bfloat16)
    delta_two = (cot[...] * slope_of(pre_two, sig)).astype(jnp.bfloat16)
    spread(delta_two.astype(jnp.float32), shift_back, 2, height, cols)
    flip_into(kernel_ref, 1, flip, channels)
    mid_grad = back_conv(shift_back, flip, 2, cells, cols) * fan_scale + cot[...]
    delta_one = (mid_grad * slope_one).astype(jnp.bfloat16)
    taps_len = 9 * channels
    map_grad(shift_two, delta_two, grad, taps_len, 2, cells, cols, channels, factor)
    map_grad(shift_one, delta_one, grad, 0, 1, cells, cols, channels, factor)
    if split:
        dp_count, piece = split
        side = lax.rem(lax.axis_index("dp"), 2)
        for layer in range(2):
            for z in range(dp_count // 2):
                spot = (layer * dp_count // 2 + z) * piece
                for out, core in ((stage, 1 - side), (keep_ref, side)):
                    start = layer * taps_len + ((2 * z + core) * count + where) * piece
                    out[spot : spot + piece, :] = grad[pl.ds(start, piece), :]
        send_ref[...] = stage[...].astype(jnp.bfloat16)
    else:
        grad_out[...] = grad[...].reshape(grad_out.shape).astype(grad_out.dtype)

    sample[...] = delta_one.astype(jnp.float32)
    flip_into(kernel_ref, 0, flip, channels)
    spread(sample[...], shift_one, 1, height, cols)
    total = None
    for a in range(3):
        start = pl.multiple_of(where * rows + a * cols, cols)
        part = lax.dot_general(
            shift_one[pl.ds(start, rows), :],
            flip[a],
            (((1,), (1,)), ((), ())),
            preferred_element_type=jnp.float32,
        )
        total = part if total is None else total + part
    input_ref[...] = (total * fan_scale).astype(jnp.bfloat16)


def vmem_call(body, outs, scratch=(), name=None, flops=0):
    spec = pl.BlockSpec(memory_space=pltpu.VMEM)

    def call(*args):
        return pl.pallas_call(
            body,
            out_shape=outs,
            in_specs=[spec] * len(args),
            out_specs=jax.tree.map(lambda _: spec, outs),
            scratch_shapes=list(scratch),
            name=name,
            cost_estimate=pl.CostEstimate(flops=flops, bytes_accessed=0, transcendentals=0),
        )(*args)

    return call


def sample_step(pieces, weights, strip, cols, split, pixel_total):
    channels = weights.shape[-1]
    count = len(pieces)
    height = count * strip
    cells = height * cols
    fan_scale = (9.0 * channels) ** (-0.5)
    factor = fan_scale * (9.0 * channels / pixel_total) ** 0.5
    rows = strip * cols
    outs = [jax.ShapeDtypeStruct((rows, channels), jnp.bfloat16)] * 2
    if split:
        length = split[0] * split[1]
        outs.append(jax.ShapeDtypeStruct((length, channels), jnp.bfloat16))
        outs.append(jax.ShapeDtypeStruct((length, channels), jnp.float32))
    else:
        length = 8
        outs.append(jax.ShapeDtypeStruct((2, 9 * channels, channels), jnp.bfloat16))
    scratch = [
        pltpu.VMEM((cells, channels), jnp.float32),
        pltpu.VMEM((cells, channels), jnp.float32),
        pltpu.VMEM((cells + 2 * cols, 3 * channels), jnp.bfloat16),
        pltpu.VMEM((cells + 4 * cols, 3 * channels), jnp.bfloat16),
        pltpu.VMEM((cells + 4 * cols, 3 * channels), jnp.bfloat16),
        pltpu.VMEM((3, channels, 3 * channels), jnp.bfloat16),
        pltpu.VMEM((cells, channels), jnp.float32),
        pltpu.VMEM((2 * 9 * channels, channels), jnp.float32),
        pltpu.VMEM((length, channels), jnp.float32),
    ]
    plan = (count, strip, cols, channels, fan_scale, factor, split)
    body = functools.partial(step_kernel, plan)
    return vmem_call(body, tuple(outs), scratch, "sample_step")(*pieces, weights)


def update_kernel(zs, piece, *refs):
    own_ref, far_ref = refs[:2]
    bases = refs[2 : 2 + zs]
    weight_ref, grad_ref, total, stage = refs[2 + zs :]
    here = lax.axis_index("dp") // 2
    total[...] = own_ref[...].astype(jnp.float32) + far_ref[...].astype(jnp.float32)
    for layer in range(2):
        for k in range(zs):
            z = here ^ k
            place = pl.ds((layer * zs + z) * piece, piece)
            value = total[place, :]
            if k == 0:
                grad_ref[layer] = value
            stage[place, :] = bases[k][layer] - learn_rate * value
    weight_ref[...] = stage[...].astype(jnp.bfloat16)


def place_kernel(zs, count, piece, *refs):
    parts, out_ref, stage, whole = (refs[:-3], refs[-3], refs[-2], refs[-1])
    where = lax.axis_index("space")
    side = lax.rem(lax.axis_index("dp"), 2)
    layer_len = zs * 2 * count * piece
    for core_flip in range(2):
        for k in range(count):
            stage[...] = parts[core_flip * count + k][...].astype(jnp.float32)
            for layer in range(2):
                for z in range(zs):
                    chunk = (2 * z + (side ^ core_flip)) * count + (where ^ k)
                    whole[pl.ds(layer * layer_len + chunk * piece, piece), :] = stage[
                        (layer * zs + z) * piece : (layer * zs + z + 1) * piece, :
                    ]
    out_ref[...] = whole[...].reshape(out_ref.shape).astype(jnp.bfloat16)


def swap(value, axis, bit):
    size = lax.axis_size(axis)
    return lax.ppermute(value, axis, [(i, i ^ bit) for i in range(size)])


def power(n):
    return n & (n - 1) == 0


def local(fields, cotangent, weights, master, momentum):
    _, strip, cols, channels = fields.shape
    layers = weights.shape[0]
    dp_count = lax.axis_size("dp")
    space_count = lax.axis_size("space")
    rows = strip * cols
    taps_len = 9 * channels
    shard_len = master.shape[1]
    pixel_total = dp_count * space_count * fields.shape[0] * rows
    pair = jnp.concatenate([fields, cotangent], axis=0).reshape(2, rows, channels)
    zs = dp_count // 2
    quick = (
        power(space_count)
        and power(dp_count)
        and 2 <= dp_count
        and zs <= space_count
        and shard_len % channels == 0
    )

    def maps(result, input_grad):
        shape = (1, strip, cols, channels)
        return result.reshape(shape), input_grad.reshape(shape)

    if not quick:
        both = lax.all_gather(pair, "space", axis=0)
        pieces = [both[k] for k in range(space_count)]
        result, input_grad, grads = sample_step(pieces, weights, strip, cols, None, pixel_total)
        blocks = grads.reshape(layers, dp_count, space_count, shard_len)
        quarter = lax.dynamic_index_in_dim(
            blocks, lax.axis_index("space"), axis=2, keepdims=False
        )
        swapped = lax.all_to_all(quarter.transpose(1, 0, 2), "dp", 0, 0, tiled=True)
        gradient = swapped.astype(jnp.float32).sum(axis=0)
        momentum_next = momentum_rate * momentum + gradient
        master_next = master - learn_rate * momentum_next
        gathered = lax.all_gather(master_next.astype(jnp.bfloat16), ("dp", "space"), axis=0)
        weights_next = gathered.transpose(1, 0, 2).reshape(layers, taps_len, channels)
        return *maps(result, input_grad), momentum_next, master_next, weights_next

    piece = shard_len // channels
    length = dp_count * piece
    base = (master - learn_rate * momentum_rate * momentum).reshape(layers, piece, channels)
    pieces = [pair] + [swap(pair, "space", k) for k in range(1, space_count)]
    bases = [base] + [swap(base, "dp", 2 * k) for k in range(1, zs)]
    split = (dp_count, piece)
    result, input_grad, send, keep = sample_step(
        pieces, weights, strip, cols, split, pixel_total
    )
    total = (keep + swap(send, "dp", 1).astype(jnp.float32)).astype(jnp.bfloat16)
    far = None
    bit = 2
    while bit < dp_count:
        far = swap(total, "dp", bit)
        bit *= 2
        if bit < dp_count:
            total = (total.astype(jnp.float32) + far.astype(jnp.float32)).astype(jnp.bfloat16)
    if far is None:
        far = jnp.zeros_like(total)
    update = vmem_call(
        functools.partial(update_kernel, zs, piece),
        (
            jax.ShapeDtypeStruct((length, channels), jnp.bfloat16),
            jax.ShapeDtypeStruct((layers, piece, channels), jnp.float32),
        ),
        [pltpu.VMEM((length, channels), jnp.float32)] * 2,
        "update",
    )
    new_piece, own_grad = update(total, far, *bases)
    near = [new_piece] + [swap(new_piece, "space", k) for k in range(1, space_count)]
    other = [swap(value, "dp", 1) for value in near]
    place = vmem_call(
        functools.partial(place_kernel, zs, space_count, piece),
        jax.ShapeDtypeStruct((layers, taps_len, channels), jnp.bfloat16),
        [
            pltpu.VMEM((length, channels), jnp.float32),
            pltpu.VMEM((layers * taps_len, channels), jnp.float32),
        ],
        "place",
    )
    weights_next = place(*near, *other)
    gradient = own_grad.reshape(layers, shard_len)
    momentum_next = momentum_rate * momentum + gradient
    master_next = master - learn_rate * momentum_next
    return *maps(result, input_grad), momentum_next, master_next, weights_next


def solution(mesh):
    split = P("dp", "space", None, None)
    shard = P(None, ("dp", "space"))
    return jax.shard_map(
        local,
        mesh=mesh,
        in_specs=(split, split, P(), shard, shard),
        out_specs=(split, split, shard, shard, P()),
        check_vma=False,
    )
```

```python
import functools

import jax
import jax.numpy as jnp
from jax import lax
from jax.experimental import pallas as pl
from jax.experimental.pallas import tpu as pltpu
from jax.sharding import PartitionSpec as P


momentum_rate = 0.9
learn_rate = 0.1


def sigmoid(value):
    return 1.0 / (1.0 + jnp.exp(-value))


def slope_of(value, sig):
    return sig * (1.0 + value * (1.0 - sig))


def spread(rows, shift_ref, dilation, height, cols):
    channels = rows.shape[-1]
    cube = rows.reshape(height, cols, channels)
    column = lax.broadcasted_iota(jnp.int32, cube.shape, 1)
    margin = dilation * cols
    right = jnp.where(column < dilation, 0.0, pltpu.roll(cube, dilation, 1))
    left = jnp.where(column >= cols - dilation, 0.0, pltpu.roll(cube, cols - dilation, 1))
    for b, moved in enumerate((right, cube, left)):
        lanes = slice(b * channels, (b + 1) * channels)
        shift_ref[margin : margin + height * cols, lanes] = moved.reshape(
            height * cols, channels
        ).astype(jnp.bfloat16)
    edge = jnp.zeros((margin, 3 * channels), jnp.bfloat16)
    shift_ref[:margin, :] = edge
    shift_ref[margin + height * cols : 2 * margin + height * cols, :] = edge


def conv(shift_ref, kernel_ref, layer, dilation, cells, cols, channels):
    total = None
    for a in range(3):
        part = jnp.dot(
            shift_ref[a * dilation * cols : a * dilation * cols + cells, :],
            kernel_ref[layer, a * 3 * channels : (a + 1) * 3 * channels, :],
            preferred_element_type=jnp.float32,
        )
        total = part if total is None else total + part
    return total


def back_conv(shift_ref, flip_ref, dilation, cells, cols):
    total = None
    for a in range(3):
        part = lax.dot_general(
            shift_ref[a * dilation * cols : a * dilation * cols + cells, :],
            flip_ref[a],
            (((1,), (1,)), ((), ())),
            preferred_element_type=jnp.float32,
        )
        total = part if total is None else total + part
    return total


def flip_into(kernel_ref, layer, flip_ref, channels):
    for a in range(3):
        for b in range(3):
            tap = ((2 - a) * 3 + (2 - b)) * channels
            flip_ref[a, :, b * channels : (b + 1) * channels] = kernel_ref[
                layer, tap : tap + channels, :
            ]


def map_grad(shift_ref, delta, grad_ref, base, dilation, cells, cols, channels, factor):
    for a in range(3):
        part = lax.dot_general(
            shift_ref[a * dilation * cols : a * dilation * cols + cells, :],
            delta,
            (((0,), (0,)), ((), ())),
            preferred_element_type=jnp.float32,
        )
        start = base + a * 3 * channels
        grad_ref[start : start + 3 * channels, :] = part * factor


def step_kernel(plan, *refs):
    count, strip, cols, channels, fan_scale, factor, split = plan
    pieces, kernel_ref = (refs[:count], refs[count])
    if split:
        result_ref, input_ref, send_ref, keep_ref = refs[count + 1 : count + 5]
        scratch = refs[count + 5 :]
    else:
        result_ref, input_ref, grad_out = refs[count + 1 : count + 4]
        scratch = refs[count + 4 :]
    sample, cot, shift_one, shift_two, shift_back, flip, pre, grad, stage = scratch
    height, rows = (count * strip, strip * cols)
    cells = height * cols
    where = lax.axis_index("space")
    for k in range(count):
        spot = (where ^ k) if split else k
        place = pl.ds(pl.multiple_of(spot * rows, rows), rows)
        sample[place, :] = pieces[k][0].astype(jnp.float32)
        cot[place, :] = pieces[k][1].astype(jnp.float32)

    spread(sample[...], shift_one, 1, height, cols)
    pre_one = conv(shift_one, kernel_ref, 0, 1, cells, cols, channels) * fan_scale
    sig = sigmoid(pre_one)
    slope_one = slope_of(pre_one, sig)
    hidden = (pre_one * sig).astype(jnp.bfloat16).astype(jnp.float32)
    sample[...] = hidden
    spread(hidden, shift_two, 2, height, cols)
    pre_two = conv(shift_two, kernel_ref, 1, 2, cells, cols, channels) * fan_scale
    sig = sigmoid(pre_two)
    pre[...] = pre_two * sig
    own = pl.ds(pl.multiple_of(where * rows, rows), rows)
    result_ref[...] = (pre[own, :] + sample[own, :]).astype(jnp.bfloat16)
    delta_two = (cot[...] * slope_of(pre_two, sig)).astype(jnp.bfloat16)
    spread(delta_two.astype(jnp.float32), shift_back, 2, height, cols)
    flip_into(kernel_ref, 1, flip, channels)
    mid_grad = back_conv(shift_back, flip, 2, cells, cols) * fan_scale + cot[...]
    delta_one = (mid_grad * slope_one).astype(jnp.bfloat16)
    taps_len = 9 * channels
    map_grad(shift_two, delta_two, grad, taps_len, 2, cells, cols, channels, factor)
    map_grad(shift_one, delta_one, grad, 0, 1, cells, cols, channels, factor)
    if split:
        dp_count, piece = split
        side = lax.rem(lax.axis_index("dp"), 2)
        for layer in range(2):
            for z in range(dp_count // 2):
                spot = (layer * dp_count // 2 + z) * piece
                for out, core in ((stage, 1 - side), (keep_ref, side)):
                    start = layer * taps_len + ((2 * z + core) * count + where) * piece
                    out[spot : spot + piece, :] = grad[pl.ds(start, piece), :]
        send_ref[...] = stage[...].astype(jnp.bfloat16)
    else:
        grad_out[...] = grad[...].reshape(grad_out.shape).astype(grad_out.dtype)

    sample[...] = delta_one.astype(jnp.float32)
    flip_into(kernel_ref, 0, flip, channels)
    spread(sample[...], shift_one, 1, height, cols)
    total = None
    for a in range(3):
        start = pl.multiple_of(where * rows + a * cols, cols)
        part = lax.dot_general(
            shift_one[pl.ds(start, rows), :],
            flip[a],
            (((1,), (1,)), ((), ())),
            preferred_element_type=jnp.float32,
        )
        total = part if total is None else total + part
    input_ref[...] = (total * fan_scale).astype(jnp.bfloat16)


def vmem_call(body, outs, scratch=(), limit=8):
    spec = pl.BlockSpec(memory_space=pltpu.VMEM)

    def call(*args):
        return pl.pallas_call(
            body,
            out_shape=outs,
            in_specs=[spec] * len(args),
            out_specs=jax.tree.map(lambda _: spec, outs),
            scratch_shapes=list(scratch),
            compiler_params=pltpu.CompilerParams(vmem_limit_bytes=limit << 20),
        )(*args)

    return call


def sample_step(pieces, weights, strip, cols, split, pixel_total):
    channels = weights.shape[-1]
    count = len(pieces)
    height = count * strip
    cells = height * cols
    fan_scale = (9.0 * channels) ** (-0.5)
    factor = fan_scale * (9.0 * channels / pixel_total) ** 0.5
    rows = strip * cols
    outs = [jax.ShapeDtypeStruct((rows, channels), jnp.bfloat16)] * 2
    if split:
        length = split[0] * split[1]
        outs.append(jax.ShapeDtypeStruct((length, channels), jnp.bfloat16))
        outs.append(jax.ShapeDtypeStruct((length, channels), jnp.float32))
    else:
        length = 8
        outs.append(jax.ShapeDtypeStruct((2, 9 * channels, channels), jnp.bfloat16))
    scratch = [
        pltpu.VMEM((cells, channels), jnp.float32),
        pltpu.VMEM((cells, channels), jnp.float32),
        pltpu.VMEM((cells + 2 * cols, 3 * channels), jnp.bfloat16),
        pltpu.VMEM((cells + 4 * cols, 3 * channels), jnp.bfloat16),
        pltpu.VMEM((cells + 4 * cols, 3 * channels), jnp.bfloat16),
        pltpu.VMEM((3, channels, 3 * channels), jnp.bfloat16),
        pltpu.VMEM((cells, channels), jnp.float32),
        pltpu.VMEM((2 * 9 * channels, channels), jnp.float32),
        pltpu.VMEM((length, channels), jnp.float32),
    ]
    plan = (count, strip, cols, channels, fan_scale, factor, split)
    body = functools.partial(step_kernel, plan)
    return vmem_call(body, tuple(outs), scratch, 20)(*pieces, weights)


def update_kernel(zs, piece, *refs):
    own_ref, far_ref = refs[:2]
    bases = refs[2 : 2 + zs]
    weight_ref, grad_ref, total, stage = refs[2 + zs :]
    here = lax.axis_index("dp") // 2
    total[...] = own_ref[...].astype(jnp.float32) + far_ref[...].astype(jnp.float32)
    for layer in range(2):
        for k in range(zs):
            z = here ^ k
            place = pl.ds((layer * zs + z) * piece, piece)
            value = total[place, :]
            if k == 0:
                grad_ref[layer] = value
            stage[place, :] = bases[k][layer] - learn_rate * value
    weight_ref[...] = stage[...].astype(jnp.bfloat16)


def place_kernel(zs, count, piece, *refs):
    parts, out_ref, stage, whole = (refs[:-3], refs[-3], refs[-2], refs[-1])
    where = lax.axis_index("space")
    side = lax.rem(lax.axis_index("dp"), 2)
    layer_len = zs * 2 * count * piece
    for core_flip in range(2):
        for k in range(count):
            stage[...] = parts[core_flip * count + k][...].astype(jnp.float32)
            for layer in range(2):
                for z in range(zs):
                    chunk = (2 * z + (side ^ core_flip)) * count + (where ^ k)
                    whole[pl.ds(layer * layer_len + chunk * piece, piece), :] = stage[
                        (layer * zs + z) * piece : (layer * zs + z + 1) * piece, :
                    ]
    out_ref[...] = whole[...].reshape(out_ref.shape).astype(jnp.bfloat16)


def swap(value, axis, bit):
    size = lax.axis_size(axis)
    return lax.ppermute(value, axis, [(i, i ^ bit) for i in range(size)])


def power(n):
    return n & (n - 1) == 0


def block(fields, cotangent, weights, master, momentum):
    _, strip, cols, channels = fields.shape
    layers = weights.shape[0]
    dp_count = lax.axis_size("dp")
    space_count = lax.axis_size("space")
    rows = strip * cols
    taps_len = 9 * channels
    shard_len = master.shape[1]
    pixel_total = dp_count * space_count * fields.shape[0] * rows
    pair = jnp.concatenate([fields, cotangent], axis=0).reshape(2, rows, channels)
    zs = dp_count // 2
    quick = (
        power(space_count)
        and power(dp_count)
        and 2 <= dp_count
        and zs <= space_count
        and shard_len % channels == 0
    )

    def maps(result, input_grad):
        shape = (1, strip, cols, channels)
        return result.reshape(shape), input_grad.reshape(shape)

    if not quick:
        both = lax.all_gather(pair, "space", axis=0)
        pieces = [both[k] for k in range(space_count)]
        result, input_grad, grads = sample_step(pieces, weights, strip, cols, None, pixel_total)
        blocks = grads.reshape(layers, dp_count, space_count, shard_len)
        quarter = lax.dynamic_index_in_dim(
            blocks, lax.axis_index("space"), axis=2, keepdims=False
        )
        swapped = lax.all_to_all(quarter.transpose(1, 0, 2), "dp", 0, 0, tiled=True)
        gradient = swapped.astype(jnp.float32).sum(axis=0)
        momentum_next = momentum_rate * momentum + gradient
        master_next = master - learn_rate * momentum_next
        gathered = lax.all_gather(master_next.astype(jnp.bfloat16), ("dp", "space"), axis=0)
        weights_next = gathered.transpose(1, 0, 2).reshape(layers, taps_len, channels)
        return *maps(result, input_grad), momentum_next, master_next, weights_next

    piece = shard_len // channels
    length = dp_count * piece
    base = (master - learn_rate * momentum_rate * momentum).reshape(layers, piece, channels)
    pieces = [pair] + [swap(pair, "space", k) for k in range(1, space_count)]
    bases = [base] + [swap(base, "dp", 2 * k) for k in range(1, zs)]
    split = (dp_count, piece)
    result, input_grad, send, keep = sample_step(pieces, weights, strip, cols, split, pixel_total)
    total = (keep + swap(send, "dp", 1).astype(jnp.float32)).astype(jnp.bfloat16)
    far = None
    bit = 2
    while bit < dp_count:
        far = swap(total, "dp", bit)
        bit *= 2
        if bit < dp_count:
            total = (total.astype(jnp.float32) + far.astype(jnp.float32)).astype(jnp.bfloat16)
    if far is None:
        far = jnp.zeros_like(total)
    update = vmem_call(
        functools.partial(update_kernel, zs, piece),
        (
            jax.ShapeDtypeStruct((length, channels), jnp.bfloat16),
            jax.ShapeDtypeStruct((layers, piece, channels), jnp.float32),
        ),
        [pltpu.VMEM((length, channels), jnp.float32)] * 2,
    )
    new_piece, own_grad = update(total, far, *bases)
    near = [new_piece] + [swap(new_piece, "space", k) for k in range(1, space_count)]
    other = [swap(value, "dp", 1) for value in near]
    place = vmem_call(
        functools.partial(place_kernel, zs, space_count, piece),
        jax.ShapeDtypeStruct((layers, taps_len, channels), jnp.bfloat16),
        [
            pltpu.VMEM((length, channels), jnp.float32),
            pltpu.VMEM((layers * taps_len, channels), jnp.float32),
        ],
    )
    weights_next = place(*near, *other)
    gradient = own_grad.reshape(layers, shard_len)
    momentum_next = momentum_rate * momentum + gradient
    master_next = master - learn_rate * momentum_next
    return *maps(result, input_grad), momentum_next, master_next, weights_next


def solution(mesh):
    split = P("dp", "space", None, None)
    shard = P(None, ("dp", "space"))
    return jax.shard_map(
        block,
        mesh=mesh,
        in_specs=(split, split, P(), shard, shard),
        out_specs=(split, split, shard, shard, P()),
        check_vma=False,
    )
```

```python
import functools

import jax
import jax.numpy as jnp
from jax import lax
from jax.experimental import pallas as pl
from jax.experimental.pallas import tpu as pltpu
from jax.sharding import PartitionSpec as P


momentum_rate = 0.9
learn_rate = 0.1
spare = 8


def sigmoid(value):
    return 1.0 / (1.0 + jnp.exp(-value))


def slope_of(value, sig):
    return sig * (1.0 + value * (1.0 - sig))


def moved(rows, steps):
    if steps == 0:
        return rows
    edge = jnp.zeros((abs(steps), rows.shape[1]), rows.dtype)
    if steps > 0:
        return jnp.concatenate([edge, rows[:-steps]], axis=0)
    return jnp.concatenate([rows[-steps:], edge], axis=0)


def spread(rows, dilation, cols):
    count, channels = rows.shape
    cube = rows.reshape(count // cols, cols, channels)
    column = lax.broadcasted_iota(jnp.int32, cube.shape, 1)
    right = jnp.where(column < dilation, 0.0, pltpu.roll(cube, dilation, 1))
    left = jnp.where(column >= cols - dilation, 0.0, pltpu.roll(cube, cols - dilation, 1))
    parts = [part.reshape(rows.shape).astype(jnp.bfloat16) for part in (right, cube, left)]
    return jnp.concatenate(parts, axis=1)


def fold(wide, dilation, cols, channels):
    total = wide[:, channels : 2 * channels]
    step = dilation * cols
    total = total + moved(wide[:, :channels], step)
    return total + moved(wide[:, 2 * channels :], -step)


def conv(shifted, kernel, dilation, cols, channels):
    wide = jnp.dot(shifted, kernel, preferred_element_type=jnp.float32)
    return fold(wide, dilation, cols, channels)


def back_conv(shifted, kernel, dilation, cols, channels):
    wide = lax.dot_general(
        shifted, kernel, (((1,), (1,)), ((), ())), preferred_element_type=jnp.float32
    )
    return fold(wide, dilation, cols, channels)


def map_grad(shifted, delta, grad_ref, base, dilation, cols, channels, factor):
    step = dilation * cols
    turned = jnp.concatenate([moved(delta, (1 - a) * -step) for a in range(3)], axis=1)
    wide = lax.dot_general(
        shifted, turned, (((0,), (0,)), ((), ())), preferred_element_type=jnp.float32
    )
    for a in range(3):
        for b in range(3):
            start = base + (a * 3 + b) * channels
            grad_ref[start : start + channels, :] = (
                wide[b * channels : (b + 1) * channels, a * channels : (a + 1) * channels]
                * factor
            )


def ahead_matrix(weight_ref, layer):
    channels = weight_ref.shape[-1]

    def tap(a, b):
        start = (a * 3 + b) * channels
        return weight_ref[layer, start : start + channels, :]

    return jnp.concatenate(
        [jnp.concatenate([tap(a, b) for a in range(3)], axis=1) for b in range(3)], axis=0
    )


def back_matrix(weight_ref, layer):
    channels = weight_ref.shape[-1]

    def tap(a, b):
        start = ((2 - a) * 3 + 2 - b) * channels
        return weight_ref[layer, start : start + channels, :]

    return jnp.concatenate(
        [jnp.concatenate([tap(a, b) for b in range(3)], axis=1) for a in range(3)], axis=0
    )


def touch_kernel(weight_ref, mark_ref):
    mark_ref[...] = jnp.zeros(mark_ref.shape, mark_ref.dtype)


def step_kernel(plan, *refs):
    count, strip, cols, channels, fan_scale, factor, split = plan
    pieces, weight_ref = (refs[:count], refs[count])
    outs, scratch = (refs[count + 2 : -6], refs[-6:])
    sample, cot, smooth, edge, grad, stage = scratch
    rows = strip * cols
    cells = count * rows
    where = lax.axis_index("space")
    for k in range(count):
        spot = (where ^ k) if split else k
        place = pl.ds(pl.multiple_of(spot * rows, rows), rows)
        sample[place, :] = pieces[k][0].reshape(rows, channels).astype(jnp.float32)
        cot[place, :] = pieces[k][1].reshape(rows, channels).astype(jnp.float32)

    one = spread(sample[...], 1, cols)
    pre_one = conv(one, ahead_matrix(weight_ref, 0), 1, cols, channels) * fan_scale
    sig = sigmoid(pre_one)
    slope_one = slope_of(pre_one, sig)
    hidden = (pre_one * sig).astype(jnp.bfloat16).astype(jnp.float32)
    two = spread(hidden, 2, cols)
    pre_two = conv(two, ahead_matrix(weight_ref, 1), 2, cols, channels) * fan_scale
    sig = sigmoid(pre_two)
    smooth[...] = pre_two * sig + hidden
    delta_two = (cot[...] * slope_of(pre_two, sig)).astype(jnp.bfloat16)
    back = spread(delta_two.astype(jnp.float32), 2, cols)
    mid_grad = back_conv(back, back_matrix(weight_ref, 1), 2, cols, channels) * fan_scale + cot[...]
    delta_one = (mid_grad * slope_one).astype(jnp.bfloat16)
    taps_len = 9 * channels
    map_grad(two, delta_two, grad, taps_len, 2, cols, channels, factor)
    map_grad(one, delta_one, grad, 0, 1, cols, channels, factor)

    edge[:cols, :] = jnp.zeros((cols, channels), jnp.bfloat16)
    edge[cols : cols + cells, :] = delta_one
    edge[cols + cells :, :] = jnp.zeros((cols, channels), jnp.bfloat16)
    start = pl.multiple_of(where * rows, rows)
    outs[0][...] = smooth[pl.ds(start, rows), :].astype(jnp.bfloat16)
    outs[1][...] = edge[pl.ds(start, rows + 2 * cols), :]
    if split:
        dp_count, piece = split
        side = lax.rem(lax.axis_index("dp"), 2)
        length = dp_count * piece
        for core in range(2):
            chosen = side if core else 1 - side
            for layer in range(2):
                for z in range(dp_count // 2):
                    spot = core * length + (layer * dp_count // 2 + z) * piece
                    start = layer * taps_len + ((2 * z + chosen) * count + where) * piece
                    stage[spot : spot + piece, :] = grad[pl.ds(start, piece), :]
        outs[2][...] = stage[:length, :].astype(jnp.bfloat16)
        outs[3][...] = stage[length : 2 * length, :]
    else:
        outs[2][...] = (
            grad[: 2 * taps_len, :].reshape(outs[2].shape).astype(outs[2].dtype)
        )


def finish_kernel(plan, smooth_ref, edge_ref, weight_ref, result_ref, input_ref):
    cols, channels, fan_scale = plan
    rows = result_ref.shape[0]
    result_ref[...] = smooth_ref[...]
    shifted = spread(edge_ref[...].astype(jnp.float32), 1, cols)
    wide = back_conv(shifted, back_matrix(weight_ref, 0), 1, cols, channels)
    input_ref[...] = (wide[cols : cols + rows, :] * fan_scale).astype(jnp.bfloat16)


def update_kernel(zs, piece, *refs):
    own_ref, far_ref = refs[:2]
    bases = refs[2 : 2 + zs]
    weight_ref, grad_ref, total, stage = refs[2 + zs :]
    here = lax.axis_index("dp") // 2
    length = own_ref.shape[0]
    total[:length, :] = own_ref[...].astype(jnp.float32) + far_ref[...].astype(jnp.float32)
    for layer in range(2):
        for k in range(zs):
            place = pl.ds((layer * zs + (here ^ k)) * piece, piece)
            value = total[place, :]
            if k == 0:
                grad_ref[layer] = value
            stage[place, :] = bases[k][layer] - learn_rate * value
    weight_ref[...] = stage[:length, :].astype(jnp.bfloat16)


def place_kernel(zs, count, piece, far, *refs):
    parts = refs[:count]
    out_ref, stage, whole, half, sems = refs[-5:]
    where = lax.axis_index("space")
    side = lax.rem(lax.axis_index("dp"), 2)
    side = 1 - side if far else side
    run = count * piece
    copies = []
    for layer in range(2):
        for k in range(count):
            rows = slice(layer * zs * piece, (layer + 1) * zs * piece)
            stage[rows, :] = parts[k][rows, :].astype(jnp.float32)
            for z in range(zs):
                spot = (layer * zs + z) * piece
                whole[pl.ds((layer * zs + z) * run + (where ^ k) * piece, piece), :] = stage[
                    spot : spot + piece, :
                ]
        for z in range(zs):
            rows = slice((layer * zs + z) * run, (layer * zs + z + 1) * run)
            half[rows, :] = whole[rows, :].astype(jnp.bfloat16)
            start = pl.multiple_of((2 * z + side) * run, run)
            copies.append(
                pltpu.make_async_copy(
                    half.at[rows],
                    out_ref.at[layer, pl.ds(start, run)],
                    sems.at[layer * zs + z],
                )
            )
            copies[-1].start()
    for copy in copies:
        copy.wait()


def place(parts, held, zs, piece, dims):
    count = len(parts)
    length = 2 * zs * piece
    channels = dims[-1]
    spec = pl.BlockSpec(memory_space=pltpu.VMEM)
    anywhere = pl.BlockSpec(memory_space=pl.ANY)
    extra = [] if held is None else [held]
    return pl.pallas_call(
        functools.partial(place_kernel, zs, count, piece, held is not None),
        out_shape=shape(dims),
        in_specs=[spec] * count + [anywhere] * len(extra),
        out_specs=anywhere,
        input_output_aliases={count: 0} if extra else {},
        scratch_shapes=[
            pltpu.VMEM((length + spare, channels), jnp.float32),
            pltpu.VMEM((count * length + spare, channels), jnp.float32),
            pltpu.VMEM((count * length, channels), jnp.bfloat16),
            pltpu.SemaphoreType.DMA((2 * zs,)),
        ],
        name="place_far" if extra else "place_near",
        compiler_params=pltpu.CompilerParams(vmem_limit_bytes=8 << 20),
    )(*parts, *extra)


def vmem_call(body, outs, scratch=(), limit=8):
    spec = pl.BlockSpec(memory_space=pltpu.VMEM)

    def call(*args):
        return pl.pallas_call(
            body,
            out_shape=outs,
            in_specs=[spec] * len(args),
            out_specs=jax.tree.map(lambda _: spec, outs),
            scratch_shapes=list(scratch),
            compiler_params=pltpu.CompilerParams(vmem_limit_bytes=limit << 20),
        )(*args)

    return call


def shape(dims, dtype=jnp.bfloat16):
    return jax.ShapeDtypeStruct(dims, dtype)


def touch(weights):
    return pl.pallas_call(
        touch_kernel,
        out_shape=shape((16, weights.shape[-1])),
        in_specs=[pl.BlockSpec(memory_space=pl.ANY)],
        out_specs=pl.BlockSpec(memory_space=pltpu.VMEM),
        name="touch",
        compiler_params=pltpu.CompilerParams(vmem_limit_bytes=54784 << 10),
    )(weights)


def sample_step(pieces, weights, mark, strip, cols, split, pixel_total):
    channels = weights.shape[-1]
    count = len(pieces)
    rows = strip * cols
    cells = count * rows
    fan_scale = (9.0 * channels) ** (-0.5)
    factor = fan_scale * (9.0 * channels / pixel_total) ** 0.5
    outs = [shape((rows, channels)), shape((rows + 2 * cols, channels))]
    length = spare
    if split:
        length = split[0] * split[1]
        outs += [shape((length, channels)), shape((length, channels), jnp.float32)]
    else:
        outs.append(shape((2, 9 * channels, channels)))
    scratch = [
        pltpu.VMEM((cells, channels), jnp.float32),
        pltpu.VMEM((cells, channels), jnp.float32),
        pltpu.VMEM((cells, channels), jnp.float32),
        pltpu.VMEM((cells + 2 * cols, channels), jnp.bfloat16),
        pltpu.VMEM((18 * channels + spare, channels), jnp.float32),
        pltpu.VMEM((2 * length + spare, channels), jnp.float32),
    ]
    plan = (count, strip, cols, channels, fan_scale, factor, split)
    body = functools.partial(step_kernel, plan)
    return vmem_call(body, tuple(outs), scratch, 24)(*pieces, weights, mark)


def finish(smooth, edge, weights, cols):
    channels = smooth.shape[-1]
    body = functools.partial(finish_kernel, (cols, channels, (9.0 * channels) ** (-0.5)))
    outs = (shape(smooth.shape), shape(smooth.shape))
    return vmem_call(body, outs, ())(smooth, edge, weights)


def swap(value, axis, bit):
    size = lax.axis_size(axis)
    return lax.ppermute(value, axis, [(i, i ^ bit) for i in range(size)])


def power(n):
    return n & (n - 1) == 0


def block(fields, cotangent, weights, master, momentum):
    _, strip, cols, channels = fields.shape
    layers = weights.shape[0]
    dp_count = lax.axis_size("dp")
    space_count = lax.axis_size("space")
    rows = strip * cols
    taps_len = 9 * channels
    shard_len = master.shape[1]
    pixel_total = dp_count * space_count * fields.shape[0] * rows
    pair = jnp.concatenate([fields, cotangent], axis=0)
    mark = touch(weights)
    zs = dp_count // 2
    quick = (
        power(space_count)
        and power(dp_count)
        and 4 <= dp_count
        and zs <= space_count
        and shard_len % channels == 0
    )

    def maps(*values):
        return [value.reshape(1, strip, cols, channels) for value in values]

    if not quick:
        both = lax.all_gather(pair, "space", axis=0)
        pieces = [both[k] for k in range(space_count)]
        smooth, edge, grads = sample_step(pieces, weights, mark, strip, cols, None, pixel_total)
        result, input_grad = finish(smooth, edge, weights, cols)
        blocks = grads.reshape(layers, dp_count, space_count, shard_len)
        quarter = lax.dynamic_index_in_dim(
            blocks, lax.axis_index("space"), axis=2, keepdims=False
        )
        swapped = lax.all_to_all(quarter.transpose(1, 0, 2), "dp", 0, 0, tiled=True)
        gradient = swapped.astype(jnp.float32).sum(axis=0)
        momentum_next = momentum_rate * momentum + gradient
        master_next = master - learn_rate * momentum_next
        gathered = lax.all_gather(master_next.astype(jnp.bfloat16), ("dp", "space"), axis=0)
        weights_next = gathered.transpose(1, 0, 2).reshape(layers, taps_len, channels)
        return *maps(result, input_grad), momentum_next, master_next, weights_next

    piece = shard_len // channels
    length = dp_count * piece
    base = (master - learn_rate * momentum_rate * momentum).reshape(layers, piece, channels)
    pieces = [pair] + [swap(pair, "space", k) for k in range(1, space_count)]
    bases = [base] + [swap(base, "dp", 2 * k) for k in range(1, zs)]
    smooth, edge, send, keep = sample_step(
        pieces, weights, mark, strip, cols, (dp_count, piece), pixel_total
    )
    total = (keep + swap(send, "dp", 1).astype(jnp.float32)).astype(jnp.bfloat16)
    bit = 2
    while bit < dp_count:
        far = swap(total, "dp", bit)
        bit *= 2
        if bit < dp_count:
            total = (total.astype(jnp.float32) + far.astype(jnp.float32)).astype(jnp.bfloat16)
    result, input_grad = finish(smooth, edge, weights, cols)
    update = vmem_call(
        functools.partial(update_kernel, zs, piece),
        (shape((length, channels)), shape((layers, piece, channels), jnp.float32)),
        [pltpu.VMEM((length + spare, channels), jnp.float32)] * 2,
    )
    new_piece, own_grad = update(total, far, *bases)
    near = [new_piece] + [swap(new_piece, "space", k) for k in range(1, space_count)]
    other = [swap(value, "dp", 1) for value in near]
    held = place(near, None, zs, piece, (layers, taps_len, channels))
    weights_next = place(other, held, zs, piece, (layers, taps_len, channels))
    gradient = own_grad.reshape(layers, shard_len)
    momentum_next = momentum_rate * momentum + gradient
    master_next = master - learn_rate * momentum_next
    return *maps(result, input_grad), momentum_next, master_next, weights_next


def solution(mesh):
    split = P("dp", "space", None, None)
    shard = P(None, ("dp", "space"))
    return jax.shard_map(
        block,
        mesh=mesh,
        in_specs=(split, split, P(), shard, shard),
        out_specs=(split, split, shard, shard, P()),
        check_vma=False,
    )
```

```python
import functools

import jax
import jax.numpy as jnp
from jax import lax
from jax.experimental import pallas as pl
from jax.experimental.pallas import tpu as pltpu
from jax.sharding import PartitionSpec as P


momentum_rate = 0.9
learn_rate = 0.1
spare = 8


def sigmoid(value):
    return 1.0 / (1.0 + jnp.exp(-value))


def slope_of(value, sig):
    return sig * (1.0 + value * (1.0 - sig))


def moved(rows, steps):
    if steps == 0:
        return rows
    edge = jnp.zeros((abs(steps), rows.shape[1]), rows.dtype)
    if steps > 0:
        return jnp.concatenate([edge, rows[:-steps]], axis=0)
    return jnp.concatenate([rows[-steps:], edge], axis=0)


def spread(rows, dilation, cols):
    count, channels = rows.shape
    cube = rows.reshape(count // cols, cols, channels)
    column = lax.broadcasted_iota(jnp.int32, cube.shape, 1)
    right = jnp.where(column < dilation, 0.0, pltpu.roll(cube, dilation, 1))
    left = jnp.where(column >= cols - dilation, 0.0, pltpu.roll(cube, cols - dilation, 1))
    parts = [part.reshape(rows.shape).astype(jnp.bfloat16) for part in (right, cube, left)]
    return jnp.concatenate(parts, axis=1)


def conv(maps, taps, dilation, cols, channels, back=False):
    step = dilation * cols
    blank = jnp.zeros((channels, channels), jnp.bfloat16)
    first = [[taps(a, b) for a in range(3)] for b in range(2)]
    second = [[taps(0, 2), blank], [taps(1, 2), taps(2, 2)]]
    right = maps[:, 2 * channels :]
    wide = mixed(maps[:, : 2 * channels], first, back)
    side = mixed(jnp.concatenate([moved(right, step), right], axis=1), second, back)
    total = wide[:, channels : 2 * channels] + side[:, :channels]
    total = total + moved(wide[:, :channels], step)
    return total + moved(wide[:, 2 * channels :] + side[:, channels:], -step)


def mixed(maps, blocks, back):
    if back:
        rows = [jnp.concatenate(column, axis=1) for column in zip(*blocks)]
        kernel = jnp.concatenate(rows, axis=0)
        dims = (((1,), (1,)), ((), ()))
    else:
        kernel = jnp.concatenate([jnp.concatenate(row, axis=1) for row in blocks], axis=0)
        dims = (((1,), (0,)), ((), ()))
    return lax.dot_general(maps, kernel, dims, preferred_element_type=jnp.float32)


def map_grad(shifted, delta, grad_ref, base, dilation, cols, channels, factor):
    step = dilation * cols
    turned = jnp.concatenate([moved(delta, (1 - a) * -step) for a in range(3)], axis=1)
    wide = lax.dot_general(
        shifted, turned, (((0,), (0,)), ((), ())), preferred_element_type=jnp.float32
    )
    for a in range(3):
        for b in range(3):
            start = base + (a * 3 + b) * channels
            grad_ref[start : start + channels, :] = (
                wide[b * channels : (b + 1) * channels, a * channels : (a + 1) * channels]
                * factor
            )


def ahead_taps(weight_ref, layer):
    channels = weight_ref.shape[-1]

    def tap(a, b):
        start = (a * 3 + b) * channels
        return weight_ref[layer, start : start + channels, :]

    return tap


def back_taps(weight_ref, layer):
    tap = ahead_taps(weight_ref, layer)
    return lambda a, b: tap(2 - a, 2 - b)


def touch_kernel(weight_ref, mark_ref):
    mark_ref[...] = jnp.zeros(mark_ref.shape, mark_ref.dtype)


def step_kernel(plan, *refs):
    count, strip, cols, channels, fan_scale, factor, split = plan
    pieces, weight_ref = (refs[:count], refs[count])
    outs, scratch = (refs[count + 2 : -6], refs[-6:])
    sample, cot, smooth, edge, grad, stage = scratch
    rows = strip * cols
    cells = count * rows
    where = lax.axis_index("space")
    for k in range(count):
        spot = (where ^ k) if split else k
        place = pl.ds(pl.multiple_of(spot * rows, rows), rows)
        sample[place, :] = pieces[k][0].reshape(rows, channels).astype(jnp.float32)
        cot[place, :] = pieces[k][1].reshape(rows, channels).astype(jnp.float32)

    one = spread(sample[...], 1, cols)
    pre_one = conv(one, ahead_taps(weight_ref, 0), 1, cols, channels) * fan_scale
    sig = sigmoid(pre_one)
    slope_one = slope_of(pre_one, sig)
    hidden = (pre_one * sig).astype(jnp.bfloat16).astype(jnp.float32)
    two = spread(hidden, 2, cols)
    pre_two = conv(two, ahead_taps(weight_ref, 1), 2, cols, channels) * fan_scale
    sig = sigmoid(pre_two)
    smooth[...] = pre_two * sig + hidden
    delta_two = (cot[...] * slope_of(pre_two, sig)).astype(jnp.bfloat16)
    back = spread(delta_two.astype(jnp.float32), 2, cols)
    mid_grad = conv(back, back_taps(weight_ref, 1), 2, cols, channels, True) * fan_scale + cot[...]
    delta_one = (mid_grad * slope_one).astype(jnp.bfloat16)
    taps_len = 9 * channels
    map_grad(two, delta_two, grad, taps_len, 2, cols, channels, factor)
    map_grad(one, delta_one, grad, 0, 1, cols, channels, factor)

    edge[:cols, :] = jnp.zeros((cols, channels), jnp.bfloat16)
    edge[cols : cols + cells, :] = delta_one
    edge[cols + cells :, :] = jnp.zeros((cols, channels), jnp.bfloat16)
    start = pl.multiple_of(where * rows, rows)
    outs[0][...] = smooth[pl.ds(start, rows), :].astype(jnp.bfloat16)
    outs[1][...] = edge[pl.ds(start, rows + 2 * cols), :]
    if split:
        dp_count, piece = split
        side = lax.rem(lax.axis_index("dp"), 2)
        length = dp_count * piece
        for core in range(2):
            chosen = side if core else 1 - side
            for layer in range(2):
                for z in range(dp_count // 2):
                    spot = core * length + (layer * dp_count // 2 + z) * piece
                    start = layer * taps_len + ((2 * z + chosen) * count + where) * piece
                    stage[spot : spot + piece, :] = grad[pl.ds(start, piece), :]
        outs[2][...] = stage[:length, :].astype(jnp.bfloat16)
        outs[3][...] = stage[length : 2 * length, :]
    else:
        outs[2][...] = (
            grad[: 2 * taps_len, :].reshape(outs[2].shape).astype(outs[2].dtype)
        )


def finish_kernel(plan, smooth_ref, edge_ref, weight_ref, result_ref, input_ref):
    cols, channels, fan_scale = plan
    rows = result_ref.shape[0]
    result_ref[...] = smooth_ref[...]
    shifted = spread(edge_ref[...].astype(jnp.float32), 1, cols)
    wide = conv(shifted, back_taps(weight_ref, 0), 1, cols, channels, True)
    input_ref[...] = (wide[cols : cols + rows, :] * fan_scale).astype(jnp.bfloat16)


def update_kernel(zs, piece, *refs):
    parts, bases = (refs[:zs], refs[zs : 2 * zs])
    weight_ref, grad_ref, pile, total, stage = refs[2 * zs :]
    here = lax.axis_index("dp") // 2
    length = parts[0].shape[0]
    for k in range(zs):
        pile[here ^ k] = parts[k][...].astype(jnp.float32)
    added = pile[0]
    for z in range(1, zs):
        added = added + pile[z]
    total[:length, :] = added
    for layer in range(2):
        for k in range(zs):
            place = pl.ds((layer * zs + (here ^ k)) * piece, piece)
            value = total[place, :]
            if k == 0:
                grad_ref[layer] = value
            stage[place, :] = bases[k][layer] - learn_rate * value
    weight_ref[...] = stage[:length, :].astype(jnp.bfloat16)


def place_kernel(zs, count, piece, far, *refs):
    parts = refs[:count]
    out_ref, stage, whole, half, sems = refs[-5:]
    where = lax.axis_index("space")
    side = lax.rem(lax.axis_index("dp"), 2)
    side = 1 - side if far else side
    run = count * piece
    copies = []
    for layer in range(2):
        for k in range(count):
            rows = slice(layer * zs * piece, (layer + 1) * zs * piece)
            stage[rows, :] = parts[k][rows, :].astype(jnp.float32)
            for z in range(zs):
                spot = (layer * zs + z) * piece
                whole[pl.ds((layer * zs + z) * run + (where ^ k) * piece, piece), :] = stage[
                    spot : spot + piece, :
                ]
        for z in range(zs):
            rows = slice((layer * zs + z) * run, (layer * zs + z + 1) * run)
            half[rows, :] = whole[rows, :].astype(jnp.bfloat16)
            start = pl.multiple_of((2 * z + side) * run, run)
            copies.append(
                pltpu.make_async_copy(
                    half.at[rows],
                    out_ref.at[layer, pl.ds(start, run)],
                    sems.at[layer * zs + z],
                )
            )
            copies[-1].start()
    for copy in copies:
        copy.wait()


def place(parts, held, zs, piece, dims):
    count = len(parts)
    length = 2 * zs * piece
    channels = dims[-1]
    spec = pl.BlockSpec(memory_space=pltpu.VMEM)
    anywhere = pl.BlockSpec(memory_space=pl.ANY)
    extra = [] if held is None else [held]
    return pl.pallas_call(
        functools.partial(place_kernel, zs, count, piece, held is not None),
        out_shape=shape(dims),
        in_specs=[spec] * count + [anywhere] * len(extra),
        out_specs=anywhere,
        input_output_aliases={count: 0} if extra else {},
        scratch_shapes=[
            pltpu.VMEM((length + spare, channels), jnp.float32),
            pltpu.VMEM((count * length + spare, channels), jnp.float32),
            pltpu.VMEM((count * length, channels), jnp.bfloat16),
            pltpu.SemaphoreType.DMA((2 * zs,)),
        ],
        name="place_far" if extra else "place_near",
        compiler_params=pltpu.CompilerParams(vmem_limit_bytes=8 << 20),
    )(*parts, *extra)


def vmem_call(body, outs, scratch=(), limit=8):
    spec = pl.BlockSpec(memory_space=pltpu.VMEM)

    def call(*args):
        return pl.pallas_call(
            body,
            out_shape=outs,
            in_specs=[spec] * len(args),
            out_specs=jax.tree.map(lambda _: spec, outs),
            scratch_shapes=list(scratch),
            compiler_params=pltpu.CompilerParams(vmem_limit_bytes=limit << 20),
        )(*args)

    return call


def shape(dims, dtype=jnp.bfloat16):
    return jax.ShapeDtypeStruct(dims, dtype)


def touch(weights):
    return pl.pallas_call(
        touch_kernel,
        out_shape=shape((16, weights.shape[-1])),
        in_specs=[pl.BlockSpec(memory_space=pl.ANY)],
        out_specs=pl.BlockSpec(memory_space=pltpu.VMEM),
        name="touch",
        compiler_params=pltpu.CompilerParams(vmem_limit_bytes=54784 << 10),
    )(weights)


def sample_step(pieces, weights, mark, strip, cols, split, pixel_total):
    channels = weights.shape[-1]
    count = len(pieces)
    rows = strip * cols
    cells = count * rows
    fan_scale = (9.0 * channels) ** (-0.5)
    factor = fan_scale * (9.0 * channels / pixel_total) ** 0.5
    outs = [shape((rows, channels)), shape((rows + 2 * cols, channels))]
    length = spare
    if split:
        length = split[0] * split[1]
        outs += [shape((length, channels)), shape((length, channels), jnp.float32)]
    else:
        outs.append(shape((2, 9 * channels, channels)))
    scratch = [
        pltpu.VMEM((cells, channels), jnp.float32),
        pltpu.VMEM((cells, channels), jnp.float32),
        pltpu.VMEM((cells, channels), jnp.float32),
        pltpu.VMEM((cells + 2 * cols, channels), jnp.bfloat16),
        pltpu.VMEM((18 * channels + spare, channels), jnp.float32),
        pltpu.VMEM((2 * length + spare, channels), jnp.float32),
    ]
    plan = (count, strip, cols, channels, fan_scale, factor, split)
    body = functools.partial(step_kernel, plan)
    return vmem_call(body, tuple(outs), scratch, 24)(*pieces, weights, mark)


def finish(smooth, edge, weights, cols):
    channels = smooth.shape[-1]
    body = functools.partial(finish_kernel, (cols, channels, (9.0 * channels) ** (-0.5)))
    outs = (shape(smooth.shape), shape(smooth.shape))
    return vmem_call(body, outs, ())(smooth, edge, weights)


def swap(value, axis, bit):
    size = lax.axis_size(axis)
    return lax.ppermute(value, axis, [(i, i ^ bit) for i in range(size)])


def power(n):
    return n & (n - 1) == 0


def block(fields, cotangent, weights, master, momentum):
    _, strip, cols, channels = fields.shape
    layers = weights.shape[0]
    dp_count = lax.axis_size("dp")
    space_count = lax.axis_size("space")
    rows = strip * cols
    taps_len = 9 * channels
    shard_len = master.shape[1]
    pixel_total = dp_count * space_count * fields.shape[0] * rows
    pair = jnp.concatenate([fields, cotangent], axis=0)
    mark = touch(weights)
    zs = dp_count // 2
    quick = (
        power(space_count)
        and power(dp_count)
        and 4 <= dp_count
        and zs <= space_count
        and shard_len % channels == 0
    )

    def maps(*values):
        return [value.reshape(1, strip, cols, channels) for value in values]

    if not quick:
        both = lax.all_gather(pair, "space", axis=0)
        pieces = [both[k] for k in range(space_count)]
        smooth, edge, grads = sample_step(pieces, weights, mark, strip, cols, None, pixel_total)
        result, input_grad = finish(smooth, edge, weights, cols)
        blocks = grads.reshape(layers, dp_count, space_count, shard_len)
        quarter = lax.dynamic_index_in_dim(
            blocks, lax.axis_index("space"), axis=2, keepdims=False
        )
        swapped = lax.all_to_all(quarter.transpose(1, 0, 2), "dp", 0, 0, tiled=True)
        gradient = swapped.astype(jnp.float32).sum(axis=0)
        momentum_next = momentum_rate * momentum + gradient
        master_next = master - learn_rate * momentum_next
        gathered = lax.all_gather(master_next.astype(jnp.bfloat16), ("dp", "space"), axis=0)
        weights_next = gathered.transpose(1, 0, 2).reshape(layers, taps_len, channels)
        return *maps(result, input_grad), momentum_next, master_next, weights_next

    piece = shard_len // channels
    length = dp_count * piece
    base = (master - learn_rate * momentum_rate * momentum).reshape(layers, piece, channels)
    pieces = [pair] + [swap(pair, "space", k) for k in range(1, space_count)]
    bases = [base] + [swap(base, "dp", 2 * k) for k in range(1, zs)]
    smooth, edge, send, keep = sample_step(
        pieces, weights, mark, strip, cols, (dp_count, piece), pixel_total
    )
    total = (keep + swap(send, "dp", 1).astype(jnp.float32)).astype(jnp.bfloat16)
    totals = [total] + [swap(total, "dp", 2 * k) for k in range(1, zs)]
    result, input_grad = finish(smooth, edge, weights, cols)
    update = vmem_call(
        functools.partial(update_kernel, zs, piece),
        (shape((length, channels)), shape((layers, piece, channels), jnp.float32)),
        [pltpu.VMEM((zs, length, channels), jnp.float32)]
        + [pltpu.VMEM((length + spare, channels), jnp.float32)] * 2,
    )
    new_piece, own_grad = update(*totals, *bases)
    near = [new_piece] + [swap(new_piece, "space", k) for k in range(1, space_count)]
    other = [swap(value, "dp", 1) for value in near]
    held = place(near, None, zs, piece, (layers, taps_len, channels))
    weights_next = place(other, held, zs, piece, (layers, taps_len, channels))
    gradient = own_grad.reshape(layers, shard_len)
    momentum_next = momentum_rate * momentum + gradient
    master_next = master - learn_rate * momentum_next
    return *maps(result, input_grad), momentum_next, master_next, weights_next


def solution(mesh):
    split = P("dp", "space", None, None)
    shard = P(None, ("dp", "space"))
    return jax.shard_map(
        block,
        mesh=mesh,
        in_specs=(split, split, P(), shard, shard),
        out_specs=(split, split, shard, shard, P()),
        check_vma=False,
    )
```

```python
import functools

import jax
import jax.numpy as jnp
from jax import lax
from jax.experimental import pallas as pl
from jax.experimental.pallas import tpu as pltpu
from jax.sharding import PartitionSpec as P


momentum_rate = 0.9
learn_rate = 0.1
spare = 8


def sigmoid(value):
    return 1.0 / (1.0 + jnp.exp(-value))


def slope_of(value, sig):
    return sig * (1.0 + value * (1.0 - sig))


def moved(rows, steps):
    if steps == 0:
        return rows
    edge = jnp.zeros((abs(steps), rows.shape[1]), rows.dtype)
    if steps > 0:
        return jnp.concatenate([edge, rows[:-steps]], axis=0)
    return jnp.concatenate([rows[-steps:], edge], axis=0)


def spread(rows, dilation, cols):
    count, channels = rows.shape
    cube = rows.reshape(count // cols, cols, channels)
    column = lax.broadcasted_iota(jnp.int32, cube.shape, 1)
    right = jnp.where(column < dilation, 0.0, pltpu.roll(cube, dilation, 1))
    left = jnp.where(column >= cols - dilation, 0.0, pltpu.roll(cube, cols - dilation, 1))
    parts = [part.reshape(rows.shape).astype(jnp.bfloat16) for part in (right, cube, left)]
    return jnp.concatenate(parts, axis=1)


def conv(maps, taps, dilation, cols, channels, back=False):
    step = dilation * cols
    blank = jnp.zeros((channels, channels), jnp.bfloat16)
    first = [[taps(a, b) for a in range(3)] for b in range(2)]
    second = [[taps(0, 2), blank], [taps(1, 2), taps(2, 2)]]
    right = maps[:, 2 * channels :]
    wide = mixed(maps[:, : 2 * channels], first, back)
    side = mixed(jnp.concatenate([moved(right, step), right], axis=1), second, back)
    total = wide[:, channels : 2 * channels] + side[:, :channels]
    total = total + moved(wide[:, :channels], step)
    return total + moved(wide[:, 2 * channels :] + side[:, channels:], -step)


def mixed(maps, blocks, back):
    if back:
        rows = [jnp.concatenate(column, axis=1) for column in zip(*blocks)]
        kernel = jnp.concatenate(rows, axis=0)
        dims = (((1,), (1,)), ((), ()))
    else:
        kernel = jnp.concatenate([jnp.concatenate(row, axis=1) for row in blocks], axis=0)
        dims = (((1,), (0,)), ((), ()))
    return lax.dot_general(maps, kernel, dims, preferred_element_type=jnp.float32)


def map_grad(shifted, delta, grad_ref, base, dilation, cols, channels, factor):
    step = dilation * cols
    turned = jnp.concatenate([moved(delta, (1 - a) * -step) for a in range(3)], axis=1)
    wide = lax.dot_general(
        shifted, turned, (((0,), (0,)), ((), ())), preferred_element_type=jnp.float32
    )
    for a in range(3):
        for b in range(3):
            start = base + (a * 3 + b) * channels
            grad_ref[start : start + channels, :] = (
                wide[b * channels : (b + 1) * channels, a * channels : (a + 1) * channels]
                * factor
            )


def ahead_taps(weight_ref, layer):
    channels = weight_ref.shape[-1]

    def tap(a, b):
        start = (a * 3 + b) * channels
        return weight_ref[layer, start : start + channels, :]

    return tap


def back_taps(weight_ref, layer):
    tap = ahead_taps(weight_ref, layer)
    return lambda a, b: tap(2 - a, 2 - b)


def touch_kernel(weight_ref, mark_ref):
    mark_ref[...] = jnp.zeros(mark_ref.shape, mark_ref.dtype)


def step_kernel(plan, *refs):
    count, strip, cols, channels, fan_scale, factor, split = plan
    pieces, weight_ref = (refs[:count], refs[count])
    outs, scratch = (refs[count + 2 : -6], refs[-6:])
    sample, cot, smooth, edge, grad, stage = scratch
    rows = strip * cols
    cells = count * rows
    where = lax.axis_index("space")
    for k in range(count):
        spot = (where ^ k) if split else k
        place = pl.ds(pl.multiple_of(spot * rows, rows), rows)
        sample[place, :] = pieces[k][0].reshape(rows, channels).astype(jnp.float32)
        cot[place, :] = pieces[k][1].reshape(rows, channels).astype(jnp.float32)

    one = spread(sample[...], 1, cols)
    pre_one = conv(one, ahead_taps(weight_ref, 0), 1, cols, channels) * fan_scale
    sig = sigmoid(pre_one)
    slope_one = slope_of(pre_one, sig)
    hidden = (pre_one * sig).astype(jnp.bfloat16).astype(jnp.float32)
    two = spread(hidden, 2, cols)
    pre_two = conv(two, ahead_taps(weight_ref, 1), 2, cols, channels) * fan_scale
    sig = sigmoid(pre_two)
    smooth[...] = pre_two * sig + hidden
    delta_two = (cot[...] * slope_of(pre_two, sig)).astype(jnp.bfloat16)
    back = spread(delta_two.astype(jnp.float32), 2, cols)
    mid_grad = conv(back, back_taps(weight_ref, 1), 2, cols, channels, True) * fan_scale + cot[...]
    delta_one = (mid_grad * slope_one).astype(jnp.bfloat16)
    taps_len = 9 * channels
    map_grad(two, delta_two, grad, taps_len, 2, cols, channels, factor)
    map_grad(one, delta_one, grad, 0, 1, cols, channels, factor)

    edge[:cols, :] = jnp.zeros((cols, channels), jnp.bfloat16)
    edge[cols : cols + cells, :] = delta_one
    edge[cols + cells :, :] = jnp.zeros((cols, channels), jnp.bfloat16)
    start = pl.multiple_of(where * rows, rows)
    outs[0][...] = smooth[pl.ds(start, rows), :].astype(jnp.bfloat16)
    outs[1][...] = edge[pl.ds(start, rows + 2 * cols), :]
    if split:
        dp_count, piece = split
        side = lax.rem(lax.axis_index("dp"), 2)
        length = dp_count * piece
        for core in range(2):
            chosen = side if core else 1 - side
            for layer in range(2):
                for z in range(dp_count // 2):
                    spot = core * length + (layer * dp_count // 2 + z) * piece
                    start = layer * taps_len + ((2 * z + chosen) * count + where) * piece
                    stage[spot : spot + piece, :] = grad[pl.ds(start, piece), :]
        outs[2][...] = stage[:length, :].astype(jnp.bfloat16)
        outs[3][...] = stage[length : 2 * length, :]
    else:
        outs[2][...] = (
            grad[: 2 * taps_len, :].reshape(outs[2].shape).astype(outs[2].dtype)
        )


def finish_kernel(plan, smooth_ref, edge_ref, weight_ref, result_ref, input_ref):
    cols, channels, fan_scale = plan
    rows = result_ref.shape[0]
    result_ref[...] = smooth_ref[...]
    shifted = spread(edge_ref[...].astype(jnp.float32), 1, cols)
    wide = conv(shifted, back_taps(weight_ref, 0), 1, cols, channels, True)
    input_ref[...] = (wide[cols : cols + rows, :] * fan_scale).astype(jnp.bfloat16)


def update_kernel(zs, piece, *refs):
    parts, bases = (refs[:zs], refs[zs : 2 * zs])
    weight_ref, grad_ref, pile, total, stage = refs[2 * zs :]
    here = lax.axis_index("dp") // 2
    length = parts[0].shape[0]
    for k in range(zs):
        pile[here ^ k] = parts[k][...].astype(jnp.float32)
    added = pile[0]
    for z in range(1, zs):
        added = added + pile[z]
    total[:length, :] = added
    for layer in range(2):
        for k in range(zs):
            place = pl.ds((layer * zs + (here ^ k)) * piece, piece)
            value = total[place, :]
            if k == 0:
                grad_ref[layer] = value
            stage[place, :] = bases[k][layer] - learn_rate * value
    weight_ref[...] = stage[:length, :].astype(jnp.bfloat16)


def place_kernel(zs, count, piece, near, far, *refs):
    parts = refs[: len(near) + len(far)]
    out_ref, stage, whole, half, sems = refs[-5:]
    where = lax.axis_index("space")
    side = lax.rem(lax.axis_index("dp"), 2)
    run = count * piece
    copies = []
    jobs = [(near, side, count)] if near else []
    if far:
        jobs.append((far, 1 - side, count // 2))
    index = 0
    for number, (flips, core, width) in enumerate(jobs):
        base = len(near) if flips is far else 0
        low = (where ^ flips[0]) // width * width
        for layer in range(2):
            for spot, flip in enumerate(flips):
                rows = slice(layer * zs * piece, (layer + 1) * zs * piece)
                stage[rows, :] = parts[base + spot][rows, :].astype(jnp.float32)
                for z in range(zs):
                    home = number * 2 * zs + layer * zs + z
                    start = ((where ^ flip) - low) * piece
                    whole[home, pl.ds(start, piece), :] = stage[
                        (layer * zs + z) * piece : (layer * zs + z + 1) * piece, :
                    ]
            for z in range(zs):
                home = number * 2 * zs + layer * zs + z
                size = width * piece
                half[home, :size, :] = whole[home, :size, :].astype(jnp.bfloat16)
                start = pl.multiple_of((2 * z + core) * run + low * piece, size)
                copies.append(
                    pltpu.make_async_copy(
                        half.at[home, pl.ds(0, size)],
                        out_ref.at[layer, pl.ds(start, size)],
                        sems.at[index],
                    )
                )
                copies[-1].start()
                index += 1
    for copy in copies:
        copy.wait()


def place(near, far, parts, held, zs, piece, count, dims):
    channels = dims[-1]
    spec = pl.BlockSpec(memory_space=pltpu.VMEM)
    anywhere = pl.BlockSpec(memory_space=pl.ANY)
    extra = [] if held is None else [held]
    homes = 2 * zs * (bool(near) + bool(far))
    return pl.pallas_call(
        functools.partial(place_kernel, zs, count, piece, near, far),
        out_shape=shape(dims),
        in_specs=[spec] * len(parts) + [anywhere] * len(extra),
        out_specs=anywhere,
        input_output_aliases={len(parts): 0} if extra else {},
        scratch_shapes=[
            pltpu.VMEM((2 * zs * piece + spare, channels), jnp.float32),
            pltpu.VMEM((homes, count * piece + spare, channels), jnp.float32),
            pltpu.VMEM((homes, count * piece, channels), jnp.bfloat16),
            pltpu.SemaphoreType.DMA((homes,)),
        ],
        name="place_far" if extra else "place_near",
        compiler_params=pltpu.CompilerParams(vmem_limit_bytes=8 << 20),
    )(*parts, *extra)


def vmem_call(body, outs, scratch=(), limit=8):
    spec = pl.BlockSpec(memory_space=pltpu.VMEM)

    def call(*args):
        return pl.pallas_call(
            body,
            out_shape=outs,
            in_specs=[spec] * len(args),
            out_specs=jax.tree.map(lambda _: spec, outs),
            scratch_shapes=list(scratch),
            compiler_params=pltpu.CompilerParams(vmem_limit_bytes=limit << 20),
        )(*args)

    return call


def shape(dims, dtype=jnp.bfloat16):
    return jax.ShapeDtypeStruct(dims, dtype)


def touch(weights):
    return pl.pallas_call(
        touch_kernel,
        out_shape=shape((16, weights.shape[-1])),
        in_specs=[pl.BlockSpec(memory_space=pl.ANY)],
        out_specs=pl.BlockSpec(memory_space=pltpu.VMEM),
        name="touch",
        compiler_params=pltpu.CompilerParams(vmem_limit_bytes=54784 << 10),
    )(weights)


def sample_step(pieces, weights, mark, strip, cols, split, pixel_total):
    channels = weights.shape[-1]
    count = len(pieces)
    rows = strip * cols
    cells = count * rows
    fan_scale = (9.0 * channels) ** (-0.5)
    factor = fan_scale * (9.0 * channels / pixel_total) ** 0.5
    outs = [shape((rows, channels)), shape((rows + 2 * cols, channels))]
    length = spare
    if split:
        length = split[0] * split[1]
        outs += [shape((length, channels)), shape((length, channels), jnp.float32)]
    else:
        outs.append(shape((2, 9 * channels, channels)))
    scratch = [
        pltpu.VMEM((cells, channels), jnp.float32),
        pltpu.VMEM((cells, channels), jnp.float32),
        pltpu.VMEM((cells, channels), jnp.float32),
        pltpu.VMEM((cells + 2 * cols, channels), jnp.bfloat16),
        pltpu.VMEM((18 * channels + spare, channels), jnp.float32),
        pltpu.VMEM((2 * length + spare, channels), jnp.float32),
    ]
    plan = (count, strip, cols, channels, fan_scale, factor, split)
    body = functools.partial(step_kernel, plan)
    return vmem_call(body, tuple(outs), scratch, 24)(*pieces, weights, mark)


def finish(smooth, edge, weights, cols):
    channels = smooth.shape[-1]
    body = functools.partial(finish_kernel, (cols, channels, (9.0 * channels) ** (-0.5)))
    outs = (shape(smooth.shape), shape(smooth.shape))
    return vmem_call(body, outs, ())(smooth, edge, weights)


def swap(value, axis, bit):
    size = lax.axis_size(axis)
    return lax.ppermute(value, axis, [(i, i ^ bit) for i in range(size)])


def power(n):
    return n & (n - 1) == 0


def block(fields, cotangent, weights, master, momentum):
    _, strip, cols, channels = fields.shape
    layers = weights.shape[0]
    dp_count = lax.axis_size("dp")
    space_count = lax.axis_size("space")
    rows = strip * cols
    taps_len = 9 * channels
    shard_len = master.shape[1]
    pixel_total = dp_count * space_count * fields.shape[0] * rows
    pair = jnp.concatenate([fields, cotangent], axis=0)
    mark = touch(weights)
    zs = dp_count // 2
    quick = (
        power(space_count)
        and power(dp_count)
        and 4 <= dp_count
        and zs <= space_count
        and shard_len % channels == 0
    )

    def maps(*values):
        return [value.reshape(1, strip, cols, channels) for value in values]

    if not quick:
        both = lax.all_gather(pair, "space", axis=0)
        pieces = [both[k] for k in range(space_count)]
        smooth, edge, grads = sample_step(pieces, weights, mark, strip, cols, None, pixel_total)
        result, input_grad = finish(smooth, edge, weights, cols)
        blocks = grads.reshape(layers, dp_count, space_count, shard_len)
        quarter = lax.dynamic_index_in_dim(
            blocks, lax.axis_index("space"), axis=2, keepdims=False
        )
        swapped = lax.all_to_all(quarter.transpose(1, 0, 2), "dp", 0, 0, tiled=True)
        gradient = swapped.astype(jnp.float32).sum(axis=0)
        momentum_next = momentum_rate * momentum + gradient
        master_next = master - learn_rate * momentum_next
        gathered = lax.all_gather(master_next.astype(jnp.bfloat16), ("dp", "space"), axis=0)
        weights_next = gathered.transpose(1, 0, 2).reshape(layers, taps_len, channels)
        return *maps(result, input_grad), momentum_next, master_next, weights_next

    piece = shard_len // channels
    length = dp_count * piece
    base = (master - learn_rate * momentum_rate * momentum).reshape(layers, piece, channels)
    pieces = [pair] + [swap(pair, "space", k) for k in range(1, space_count)]
    bases = [base] + [swap(base, "dp", 2 * k) for k in range(1, zs)]
    smooth, edge, send, keep = sample_step(
        pieces, weights, mark, strip, cols, (dp_count, piece), pixel_total
    )
    total = (keep + swap(send, "dp", 1).astype(jnp.float32)).astype(jnp.bfloat16)
    totals = [total] + [swap(total, "dp", 2 * k) for k in range(1, zs)]
    result, input_grad = finish(smooth, edge, weights, cols)
    update = vmem_call(
        functools.partial(update_kernel, zs, piece),
        (shape((length, channels)), shape((layers, piece, channels), jnp.float32)),
        [pltpu.VMEM((zs, length, channels), jnp.float32)]
        + [pltpu.VMEM((length + spare, channels), jnp.float32)] * 2,
    )
    new_piece, own_grad = update(*totals, *bases)
    near = [new_piece] + [swap(new_piece, "space", k) for k in range(1, space_count)]
    other = [swap(value, "dp", 1) for value in near]
    dims = (layers, taps_len, channels)
    every = tuple(range(space_count))
    early, late = (every[space_count // 2 :], every[: space_count // 2])
    held = place(every, early, near + other[space_count // 2 :], None, zs, piece, space_count, dims)
    weights_next = place((), late, other[: space_count // 2], held, zs, piece, space_count, dims)
    gradient = own_grad.reshape(layers, shard_len)
    momentum_next = momentum_rate * momentum + gradient
    master_next = master - learn_rate * momentum_next
    return *maps(result, input_grad), momentum_next, master_next, weights_next


def solution(mesh):
    split = P("dp", "space", None, None)
    shard = P(None, ("dp", "space"))
    return jax.shard_map(
        block,
        mesh=mesh,
        in_specs=(split, split, P(), shard, shard),
        out_specs=(split, split, shard, shard, P()),
        check_vma=False,
    )
```
